512 devices in a mesh: seq: 64 (over z, x, core), mlp: 8 (over y).
Axes of the slice: x: 4, y: 8, z: 8, core: 2. Of those that a mesh axis runs over, the one named last changes fastest.
Arguments:
- tokens: bfloat16 [4, 48, 2048], P(None, None, 'seq'), may hold values from -20 to 20
- lengths: int32 [48], replicated, may hold values from 1 to 8192, 48960 in all
- slopes: float32 [16], P('mlp'), may hold values from 1.5258789e-05 to 0.0625
- ln1_gain: float32 [2048], P('seq'), may hold values from 0.1 to 1.9
- ln1_bias: float32 [2048], P('seq'), may hold values from -3 to 3
- w_qkv: bfloat16 [2048, 6144], P('seq', 'mlp'), may hold values from -0.125 to 0.125
- b_qkv: float32 [6144], P('mlp'), may hold values from -3 to 3
- keys: bfloat16 [65536, 2048], P('seq', 'mlp'), may hold values from -200 to 200
- values: bfloat16 [65536, 2048], P('seq', 'mlp'), may hold values from -5 to 5
- w_dense: bfloat16 [2048, 2048], P('mlp', 'seq'), may hold values from -0.125 to 0.125
- b_dense: float32 [2048], P('seq'), may hold values from -2 to 2
- ln2_gain: float32 [2048], P('seq'), may hold values from 0.1 to 1.9
- ln2_bias: float32 [2048], P('seq'), may hold values from -3 to 3
- w_up: bfloat16 [2048, 8192], P('seq', 'mlp'), may hold values from -0.125 to 0.125
- b_up: float32 [8192], P('mlp'), may hold values from -3 to 3
- w_down: bfloat16 [8192, 2048], P('mlp', 'seq'), may hold values from -0.0625 to 0.0625
- b_down: float32 [2048], P('seq'), may hold values from -2 to 2
Outputs:
- attended: bfloat16 [4, 48, 2048], P(None, None, 'seq')
- mixed: bfloat16 [4, 48, 2048], P(None, None, 'seq')
The draws below stay inside these ranges and needn't reach their ends.
Inputs may be any that keep to these rules, and one draw needn't show every extreme that they name: `lengths`: slots after the last request's 4 drafted slots hold no request's data.
All inputs are finite; a program needn't handle non-finite values.
Results may differ from the reference program's by a relative error of at most 0.008.
The reference program's roundings to bfloat16 on the way count: a program that leaves them out, or rounds other values in their place, can miss the bound.
Values may be sent and summed in bfloat16 or wider, within the bound.
A program may use at most 64 MiB of HBM per device.

```python
import math
import jax
import jax.numpy as jnp
import numpy as np
from jax import lax

D = 2048
H = 16
HD = 128
FF = 8192
REQ = 48
STEPS = 4
SLOTS = 1024
CAP = 65536
MAXLEN = 8192
FILLED = 49152


def draw_tokens(key, part):
    noise_key, rough_key, row_key = jax.random.split(key, 3)
    column = jnp.arange(D, dtype=jnp.float32) / D
    rough = jnp.exp(jax.random.uniform(rough_key, (D,), jnp.float32, 0.0, math.log(3.3)))
    column_scale = 0.25 * jnp.exp(math.log(3.0) * column) * rough
    row_scale = jnp.exp(jax.random.uniform(row_key, (STEPS, REQ, 1), jnp.float32, math.log(0.3), math.log(2.0)))
    base = jnp.clip(jax.random.normal(noise_key, (STEPS, REQ, D), jnp.float32), -4.0, 4.0)
    return (base * row_scale * column_scale).astype(jnp.bfloat16)


def draw_slopes(key, part):
    slow_key = jax.random.fold_in(key, 1)
    return jnp.exp(jax.random.uniform(slow_key, (H,), jnp.float32, math.log(1.0 / (2.0 * MAXLEN)), math.log(1.0 / 16.0)))


def draw_keys(key, part):
    noise_key = jax.random.fold_in(key, 0)
    base = jnp.clip(jax.random.normal(noise_key, (CAP, D), jnp.float32), -5.0, 5.0)
    return base.astype(jnp.bfloat16)


def steps_of(rng, shape, shards, least, high):
    level = 1.0
    for dim, blocks in shards:
        draws = jax.random.uniform(jax.random.fold_in(jax.random.fold_in(rng, 6), dim), (blocks,), jnp.float32, least / len(shards), high / len(shards))
        level = level * jnp.repeat(jnp.exp(draws), shape[dim] // blocks).reshape((-1,) + (1,) * (len(shape) - 1 - dim))
    return level


def split_up(amount, total, most, slope):
    weights = [(1 << 20) // math.isqrt(grade ** slope) + 1 for grade in range(2, amount + 1)]
    spare, holding = total - most - (amount - 1), [1] * (amount - 1)
    while spare > 0:
        free = [i for i in range(amount - 1) if holding[i] < most]
        whole, remaining = sum([weights[i] for i in free]), spare
        for i in free:
            extra = min(most - holding[i], max(1, remaining * weights[i] // whole), spare)
            holding[i] = holding[i] + extra
            spare = spare - extra
    return np.array([most] + holding)


def ragged_sizes(own_key, number_of, total, limit, skew):
    if number_of == 2:
        one = jax.random.randint(own_key, (), max(1, total - limit), min(limit, total - 1) + 1)
        return jnp.stack([one, total - one])
    tallies = jnp.asarray(split_up(number_of, total, limit, skew), jnp.int32)
    couples = (number_of - 1) // 2
    donor, receiver = tallies[1:1 + 2 * couples:2], tallies[2:2 + 2 * couples:2]
    margin = jnp.minimum(donor - 1, limit - receiver)
    moved = jax.random.randint(jax.random.fold_in(own_key, 1), (couples,), 0, 1 << 20) % (margin + 1)
    tallies = tallies.at[1:1 + 2 * couples:2].set(donor - moved).at[2:2 + 2 * couples:2].set(receiver + moved)
    return tallies[jax.random.permutation(jax.random.fold_in(own_key, 2), number_of)]


def centred(stream_key, shape, width, bound, pieces=(), kind=jnp.bfloat16):
    loudness = steps_of(stream_key, shape, pieces, -0.22, 0.18) if pieces else 1.0
    values = jax.random.normal(stream_key, shape, jnp.float32) * width * loudness
    return jnp.minimum(jnp.maximum(values, -bound), bound).astype(kind)


def setup_inputs(seed: int = 0) -> dict:
    arg_keys = jax.random.split(jax.random.key(seed), 18)
    tokens = draw_tokens(jax.random.fold_in(arg_keys[17], 71), 0)
    lengths = ragged_sizes(arg_keys[1], REQ, FILLED - STEPS * REQ, MAXLEN, 2).astype(jnp.int32)
    slopes = draw_slopes(jax.random.fold_in(arg_keys[17], 71), 0)
    ln1_gain = jnp.clip(1.0 + 0.18 * jax.random.normal(arg_keys[3], (D,), jnp.float32), 0.1, 1.9)
    ln1_bias = centred(arg_keys[4], (D,), 0.5, 3.0, ((0, 64),), jnp.float32)
    w_qkv = centred(arg_keys[5], (D, 3 * D), D ** -0.5, 0.125, ((0, 64), (1, 8)))
    b_qkv = centred(arg_keys[6], (3 * D,), 0.5, 3.0, ((0, 8),), jnp.float32)
    keys = draw_keys(jax.random.fold_in(arg_keys[17], 71), 0)
    values = centred(arg_keys[8], (CAP, D), 1.0, 5.0, ((0, 64), (1, 8)))
    w_dense = centred(arg_keys[9], (D, D), D ** -0.5, 0.125, ((0, 8), (1, 64)))
    b_dense = centred(arg_keys[10], (D,), 0.3, 2.0, ((0, 64),), jnp.float32)
    ln2_gain = jnp.clip(1.0 + 0.18 * jax.random.normal(arg_keys[11], (D,), jnp.float32), 0.1, 1.9)
    ln2_bias = centred(arg_keys[12], (D,), 0.5, 3.0, ((0, 64),), jnp.float32)
    w_up = centred(arg_keys[13], (D, FF), D ** -0.5, 0.125, ((0, 64), (1, 8)))
    b_up = centred(arg_keys[14], (FF,), 0.5, 3.0, ((0, 8),), jnp.float32)
    w_down = centred(arg_keys[15], (FF, D), FF ** -0.5, 0.0625, ((0, 8), (1, 64)))
    b_down = centred(arg_keys[16], (D,), 0.3, 2.0, ((0, 64),), jnp.float32)
    return dict(tokens=tokens, lengths=lengths, slopes=slopes, ln1_gain=ln1_gain, ln1_bias=ln1_bias, w_qkv=w_qkv, b_qkv=b_qkv, keys=keys, values=values, w_dense=w_dense, b_dense=b_dense, ln2_gain=ln2_gain, ln2_bias=ln2_bias, w_up=w_up, b_up=b_up, w_down=w_down, b_down=b_down)


NEG = -1e+30
EPS = 1e-05

def normalize(rows, gain, shift):
    mean = lax.optimization_barrier(jnp.mean(rows, axis=-1, keepdims=True))
    second = lax.optimization_barrier(jnp.mean(rows * rows, axis=-1, keepdims=True))
    spread = second - mean * mean
    return ((rows - mean) * lax.rsqrt(spread + EPS) * gain + shift).astype(jnp.bfloat16)

def gelu_tanh(value):
    return 0.5 * value * (1.0 + jnp.tanh(0.7978845608028654 * (value + 0.044715 * value * value * value)))

def reference(tokens, lengths, slopes, ln1_gain, ln1_bias, w_qkv, b_qkv, keys, values, w_dense, b_dense, ln2_gain, ln2_bias, w_up, b_up, w_down, b_down):
    spans = lengths + STEPS
    starts = (jnp.cumsum(spans) - spans).astype(jnp.int32)
    inputs = tokens.astype(jnp.float32)
    normed = normalize(inputs, ln1_gain, ln1_bias)
    projected = jnp.dot(normed.reshape(STEPS * REQ, D), w_qkv, preferred_element_type=jnp.float32) + b_qkv
    projected = projected.reshape(STEPS, REQ, H, 3, HD)
    queries = projected[:, :, :, 0, :].astype(jnp.bfloat16).reshape(STEPS, REQ, D)
    new_keys = projected[:, :, :, 1, :].astype(jnp.bfloat16).reshape(STEPS * REQ, D)
    new_values = projected[:, :, :, 2, :].astype(jnp.bfloat16).reshape(STEPS * REQ, D)
    targets = ((starts + lengths)[None, :] + jnp.arange(STEPS, dtype=jnp.int32)[:, None]).reshape(-1)
    keys = keys.at[targets].set(new_keys)
    values = values.at[targets].set(new_values)
    block = SLOTS
    outputs = []
    for step in range(STEPS):

        def visit(carry, index):
            maxima, totals, weighted = carry
            first = (index * block).astype(jnp.int32)
            positions = first + jnp.arange(block, dtype=jnp.int32)
            key_rows = lax.dynamic_slice_in_dim(keys, first, block, 0).astype(jnp.float32).reshape(block, H, HD)
            value_rows = lax.dynamic_slice_in_dim(values, first, block, 0).astype(jnp.float32).reshape(block, H, HD)
            owner = lax.optimization_barrier(jnp.sum((starts[None, :] <= positions[:, None]).astype(jnp.int32), axis=1)) - 1
            owner = jnp.clip(owner, 0, REQ - 1).astype(jnp.int32)
            offset = positions - starts[owner]
            reach = lengths[owner] + step
            valid = offset <= reach
            picked = queries[step][owner].astype(jnp.float32).reshape(block, H, HD)
            scores = lax.optimization_barrier(jnp.sum(picked * key_rows, axis=-1)) / math.sqrt(HD)
            scores = scores - slopes[None, :] * (reach - offset).astype(jnp.float32)[:, None]
            scores = jnp.where(valid[:, None], scores, NEG)
            local = jax.ops.segment_max(scores, owner, num_segments=REQ)
            fresh = jnp.maximum(maxima, local)
            weights = jnp.where(valid[:, None], jnp.exp(scores - fresh[owner]), 0.0)
            decay = jnp.exp(maxima - fresh)
            totals = totals * decay + jax.ops.segment_sum(weights, owner, num_segments=REQ)
            weighted = weighted * decay[:, :, None] + jax.ops.segment_sum(weights[:, :, None] * value_rows, owner, num_segments=REQ)
            return ((fresh, totals, weighted), None)
        start = (jnp.full((REQ, H), NEG, jnp.float32), jnp.zeros((REQ, H), jnp.float32), jnp.zeros((REQ, H, HD), jnp.float32))
        (maxima, totals, weighted), unused = lax.scan(visit, start, jnp.arange(CAP // block, dtype=jnp.int32))
        outputs.append((weighted / totals[:, :, None]).astype(jnp.bfloat16).reshape(REQ, D))
    attention = jnp.stack(outputs).reshape(STEPS * REQ, D)
    dense = jnp.dot(attention, w_dense, preferred_element_type=jnp.float32) + b_dense
    attended = dense.astype(jnp.bfloat16).reshape(STEPS, REQ, D)
    hidden = (inputs.reshape(STEPS * REQ, D) + dense).astype(jnp.bfloat16)
    hidden_full = hidden.astype(jnp.float32)
    normed_second = normalize(hidden_full, ln2_gain, ln2_bias)
    upward = jnp.dot(normed_second, w_up, preferred_element_type=jnp.float32) + b_up
    activated = gelu_tanh(upward).astype(jnp.bfloat16)
    downward = jnp.dot(activated, w_down, preferred_element_type=jnp.float32) + b_down
    mixed = (hidden_full + downward).astype(jnp.bfloat16).reshape(STEPS, REQ, D)
    return (attended, mixed)
```

```python
import math

import jax
import jax.numpy as jnp
from jax import lax
from jax.experimental import pallas as pl
from jax.experimental.pallas import tpu as pltpu
from jax.sharding import PartitionSpec as P

HD = 128
STEPS = 4
GROUP = 8
ROWS = 24
LANES = 128
NEG = -1e30
FLOOR = -1e29
EPS = 1e-05
MESH = pl.DeviceIdType.MESH

F32 = jnp.float32
BF16 = jnp.bfloat16
NT = (((1,), (1,)), ((), ()))


def gelu_tanh(value):
    return (
        0.5
        * value
        * (1.0 + jnp.tanh(0.7978845608028654 * (value + 0.044715 * value * value * value)))
    )


def dot(a, b):
    return jnp.dot(a, b, preferred_element_type=F32)


def dot_nt(a, b):
    return lax.dot_general(a, b, NT, preferred_element_type=F32)


def iota(shape, dim):
    return lax.broadcasted_iota(jnp.int32, shape, dim)


def to_row(columns):
    lane, row = iota((ROWS, LANES), 1), iota((ROWS, LANES), 0)
    packed = jnp.zeros((ROWS, LANES), F32)
    for i, column in enumerate(columns):
        packed = jnp.where(lane == row + 32 * i, column, packed)
    return jnp.sum(packed, axis=0, keepdims=True)


def to_column(row, i):
    lane, place = iota((ROWS, LANES), 1), iota((ROWS, LANES), 0)
    return jnp.sum(jnp.where(lane == place + 32 * i, row, 0.0), axis=1, keepdims=True)


def kernel(
    features,
    tokens,
    lengths,
    slopes,
    ln1_gain,
    ln1_bias,
    w_qkv,
    b_qkv,
    keys,
    values,
    w_dense,
    b_dense,
    ln2_gain,
    ln2_bias,
    w_up,
    b_up,
    w_down,
    b_down,
    attended_out,
    mixed_out,
    x_send,
    x_recv,
    vec_rows,
    vec_send,
    vec_recv,
    qkv_full,
    dense_full,
    up_full,
    down_full,
    stat_send,
    stat_recv,
    part_qkv,
    sum_qkv,
    own_qkv,
    all_qkv,
    q_all,
    bias,
    score,
    weight,
    o_send,
    ml_send,
    o_recv,
    ml_recv,
    oz_recv,
    mlz_recv,
    dense_recv,
    att_send,
    att_recv,
    stat2_send,
    stat2_recv,
    part_up,
    sum_up,
    own_act,
    all_act,
    down_recv,
    mix_send,
    mix_recv,
    send_sem,
    recv_sem,
):
    rows = ROWS * GROUP
    requests = lengths.shape[1]
    slot_count = keys.shape[0]
    s = lax.axis_index("seq")
    y = lax.axis_index("mlp")
    z, a = s // GROUP, lax.rem(s, GROUP)

    def in_a(k):
        peer = lax.rem(a + k, GROUP)
        return peer, (z * GROUP + peer, y)

    def in_z(k):
        peer = lax.rem(z + k, GROUP)
        return peer, (peer * GROUP + a, y)

    def in_y(k):
        peer = lax.rem(y + k, GROUP)
        return peer, (s, peer)

    barrier = pltpu.get_barrier_semaphore()
    for ring in (in_a, in_z, in_y):
        for k in range(1, GROUP):
            pl.semaphore_signal(barrier, inc=1, device_id=ring(k)[1], device_id_type=MESH)

    started = []

    def exchange(stage, ring, source, target, me):
        copies = []
        for k in range(1, GROUP):
            peer, device = ring(k)
            copy = pltpu.make_async_remote_copy(
                src_ref=source(peer),
                dst_ref=target(me),
                send_sem=send_sem.at[stage, k],
                recv_sem=recv_sem.at[stage, k],
                device_id=device,
                device_id_type=MESH,
            )
            copy.start()
            copies.append(copy)
        started.extend(copies)

        def arrived():
            for copy in copies:
                copy.wait_recv()

        return arrived

    quarter = lax.rem(a, 4)
    spread = (iota((32, LANES), 1) == iota((32, LANES), 0) + 32 * quarter).astype(BF16)
    mine = jnp.zeros((rows, 32), F32)
    for t in range(STEPS):
        pick = (iota((rows, requests), 0) == STEPS * iota((rows, requests), 1) + t).astype(BF16)
        mine += dot_nt(pick, tokens[t])
    placed = dot(mine.astype(BF16), spread).astype(BF16).astype(F32)
    for b in range(GROUP):
        x_send[b] = placed[ROWS * b : ROWS * (b + 1)].astype(BF16)
    x_recv[a] = x_send[a]

    vec_rows[...] = jnp.zeros_like(vec_rows)
    for i, ref in enumerate((ln1_gain, ln1_bias, ln2_gain, ln2_bias, b_dense, b_down)):
        vec_rows[i : i + 1, :] = ref[...]
    vec_send[...] = jnp.dot(
        vec_rows[...],
        (iota((32, LANES), 1) == iota((32, LANES), 0) + 32 * quarter).astype(F32),
        preferred_element_type=F32,
        precision=lax.Precision.HIGHEST,
    )
    vec_recv[a] = vec_send[...]

    def block_of(ref):
        def at(i):
            return ref.at[pl.ds(pl.multiple_of(i * 32, 32), 32), :]

        return at

    qkv_full[pl.ds(pl.multiple_of(a * 32, 32), 32), :] = w_qkv[...]
    dense_full[pl.ds(pl.multiple_of(a * 32, 32), 32), :] = w_dense[...]
    up_full[pl.ds(pl.multiple_of(a * 32, 32), 32), :] = w_up[...]
    down_full[pl.ds(pl.multiple_of(a * 32, 32), 32), :] = w_down[...]

    pl.semaphore_wait(barrier, 3 * (GROUP - 1))

    x_here = exchange(0, in_a, lambda p: x_send.at[p], lambda m: x_recv.at[m], a)
    vec_here = exchange(1, in_a, lambda p: vec_send, lambda m: vec_recv.at[m], a)
    qkv_here = exchange(2, in_a, lambda p: w_qkv, block_of(qkv_full), a)
    dense_here = exchange(3, in_a, lambda p: w_dense, block_of(dense_full), a)
    up_here = exchange(4, in_a, lambda p: w_up, block_of(up_full), a)
    down_here = exchange(5, in_a, lambda p: w_down, block_of(down_full), a)

    def halves(slots):
        low = slots[0].astype(F32)
        high = slots[4].astype(F32)
        for i in range(1, 4):
            low = low + slots[i].astype(F32)
            high = high + slots[4 + i].astype(F32)
        return jnp.concatenate([low, high], axis=1)

    def statistics(tile):
        return to_row(
            [jnp.sum(tile, axis=1, keepdims=True), jnp.sum(tile * tile, axis=1, keepdims=True)]
        )

    def add_slots(slots):
        total = slots[0]
        for i in range(1, GROUP):
            total = total + slots[i]
        return total

    def normalize(tile, stats, gain, shift):
        mean = to_column(stats, 0) / features
        spread = to_column(stats, 1) / features - mean * mean
        return ((tile - mean) * lax.rsqrt(spread + EPS) * gain + shift).astype(BF16)

    x_here()
    x = halves(x_recv)
    stat_send[...] = statistics(x)
    stat_recv[z] = stat_send[...]
    stat_here = exchange(6, in_z, lambda p: stat_send, lambda m: stat_recv.at[m], z)

    half = 32
    position = (s * slot_count + iota((1, slot_count), 1)).astype(F32)
    for c in range(rows // half):
        row = iota((half, 1), 0) + half * c
        request, step = row >> 2, (row & 3).astype(F32)
        lane = iota((half, requests), 1)
        cached = jnp.broadcast_to(lengths[...], (half, requests)).astype(F32)
        start = jnp.sum(jnp.where(lane < request, cached + STEPS, 0.0), axis=1, keepdims=True)
        length = jnp.sum(jnp.where(lane == request, cached, 0.0), axis=1, keepdims=True)
        offset = position - start
        valid = (offset >= 0.0) & (offset < length)
        distance = (length + step) - offset
        for h in range(2):
            bias[h, half * c : half * (c + 1), :] = jnp.where(valid, -slopes[h] * distance, NEG)

    vec_here()
    vectors = halves(vec_recv)
    stat_here()
    normed = normalize(x, add_slots(stat_recv), vectors[0:1], vectors[1:2])

    qkv_here()
    partial = dot(normed, qkv_full[...])
    for j in range(6):
        part_qkv[j] = partial[:, LANES * j : LANES * (j + 1)]
    for j in range(6, GROUP):
        part_qkv[j] = jnp.zeros((ROWS, LANES), F32)
    sum_qkv[z] = part_qkv[z]
    exchange(7, in_z, lambda p: part_qkv.at[p], lambda m: sum_qkv.at[m], z)()
    own_qkv[...] = (add_slots(sum_qkv) + b_qkv[pl.ds(z, 1), :]).astype(BF16)
    all_qkv[z] = own_qkv[...]
    exchange(8, in_z, lambda p: own_qkv, lambda m: all_qkv.at[m], z)()
    for h in range(2):
        q_all[h, a] = all_qkv[3 * h]
    q0_here = exchange(9, in_a, lambda p: all_qkv.at[0], lambda m: q_all.at[0, m], a)
    q1_here = exchange(10, in_a, lambda p: all_qkv.at[3], lambda m: q_all.at[1, m], a)

    scale = 1.0 / math.sqrt(HD)
    fresh = []
    one, other = iota((ROWS, ROWS), 0), iota((ROWS, ROWS), 1)
    seen = ((one >> 2) == (other >> 2)) & ((other & 3) <= (one & 3))
    gap = ((one & 3) - (other & 3)).astype(F32)
    for h in range(2):
        near = dot_nt(all_qkv[3 * h], all_qkv[3 * h + 1]) * scale - slopes[h] * gap
        near = jnp.where(seen, near, NEG)
        top = jnp.max(near, axis=1, keepdims=True)
        share = jnp.exp(near - top)
        fresh.append(
            (dot(share.astype(BF16), all_qkv[3 * h + 2]), top, jnp.sum(share, axis=1, keepdims=True))
        )

    maxima, totals = [], []
    for h in range(2):
        (q0_here, q1_here)[h]()
        query = q_all[h].astype(F32).reshape(rows, HD).astype(BF16)
        score[...] = dot_nt(query, keys[:, HD * h : HD * (h + 1)])
        tops, sums = [], []
        for c in range(rows // half):
            span = slice(half * c, half * (c + 1))
            value = score[span, :] * scale + bias[h, span, :]
            top = jnp.maximum(jnp.max(value, axis=1, keepdims=True), FLOOR)
            share = jnp.exp(value - top)
            weight[span, :] = share.astype(BF16)
            tops.append(top)
            sums.append(jnp.sum(share, axis=1, keepdims=True))
        maxima.append(jnp.concatenate(tops, axis=0))
        totals.append(jnp.concatenate(sums, axis=0))
        out = dot(weight[...], values[:, HD * h : HD * (h + 1)])
        for b in range(GROUP):
            o_send[b, :, HD * h : HD * (h + 1)] = out[ROWS * b : ROWS * (b + 1)]
    for b in range(GROUP):
        span = slice(ROWS * b, ROWS * (b + 1))
        ml_send[b] = to_row([maxima[0][span], maxima[1][span], totals[0][span], totals[1][span]])
    o_recv[a] = o_send[a]
    ml_recv[a] = ml_send[a]
    ml_here = exchange(11, in_a, lambda p: ml_send.at[p], lambda m: ml_recv.at[m], a)
    o_here = exchange(12, in_a, lambda p: o_send.at[p], lambda m: o_recv.at[m], a)

    def combine(parts):
        top = parts[0][1]
        for part in parts[1:]:
            top = jnp.maximum(top, part[1])
        weighted, total = 0.0, 0.0
        for value, largest, amount in parts:
            factor = jnp.exp(largest - top)
            weighted = weighted + value * factor
            total = total + amount * factor
        return weighted, top, total

    def slots_of(o_ref, ml_ref, h):
        return [
            (
                o_ref[i, :, HD * h : HD * (h + 1)],
                to_column(ml_ref[i], h),
                to_column(ml_ref[i], 2 + h),
            )
            for i in range(GROUP)
        ]

    ml_here()
    o_here()
    merged = [combine(slots_of(o_recv, ml_recv, h)) for h in range(2)]
    for h in range(2):
        oz_recv[z, :, HD * h : HD * (h + 1)] = merged[h][0]
    mlz_recv[z] = to_row([merged[0][1], merged[1][1], merged[0][2], merged[1][2]])
    ml_here = exchange(13, in_z, lambda p: mlz_recv.at[z], lambda m: mlz_recv.at[m], z)
    o_here = exchange(14, in_z, lambda p: oz_recv.at[z], lambda m: oz_recv.at[m], z)
    ml_here()
    o_here()
    attention = []
    for h in range(2):
        weighted, _, total = combine(slots_of(oz_recv, mlz_recv, h) + [fresh[h]])
        attention.append((weighted / total).astype(BF16))
    attention = jnp.concatenate(attention, axis=1)

    dense_here()
    dense_recv[y] = dot_nt(attention, dense_full[...])
    exchange(15, in_y, lambda p: dense_recv.at[y], lambda m: dense_recv.at[m], y)()
    dense = add_slots(dense_recv) + vectors[4:5]
    hidden = (x + dense).astype(BF16).astype(F32)
    stat2_send[...] = statistics(hidden)
    stat2_recv[z] = stat2_send[...]
    stat2_here = exchange(16, in_z, lambda p: stat2_send, lambda m: stat2_recv.at[m], z)
    for i in range(2):
        att_send[i] = dense[:, LANES * i : LANES * (i + 1)].astype(BF16)
    att_recv[a] = att_send[a // 4]
    att_here = exchange(17, in_a, lambda p: att_send.at[p // 4], lambda m: att_recv.at[m], a)
    stat2_here()
    normed = normalize(hidden, add_slots(stat2_recv), vectors[2:3], vectors[3:4])

    up_here()
    partial = dot(normed, up_full[...])
    for j in range(GROUP):
        part_up[j] = partial[:, LANES * j : LANES * (j + 1)]
    sum_up[z] = part_up[z]
    exchange(18, in_z, lambda p: part_up.at[p], lambda m: sum_up.at[m], z)()
    own_act[...] = gelu_tanh(add_slots(sum_up) + b_up[pl.ds(z, 1), :]).astype(BF16)
    all_act[z] = own_act[...]
    act_here = exchange(19, in_z, lambda p: own_act, lambda m: all_act.at[m], z)

    def deliver(slots, out_ref):
        held = jnp.concatenate([slots[i].astype(F32) for i in range(GROUP)], axis=0)
        own = dot_nt(spread, held.astype(BF16)).astype(BF16)
        for t in range(STEPS):
            put = iota((rows, requests), 0) == STEPS * iota((rows, requests), 1) + t
            out_ref[t] = dot(own, put.astype(BF16)).astype(BF16)

    att_here()
    deliver(att_recv, attended_out)

    down_here()
    act_here()
    act = jnp.concatenate([all_act[i] for i in range(GROUP)], axis=1)
    down_recv[y] = dot_nt(act, down_full[...])
    exchange(20, in_y, lambda p: down_recv.at[y], lambda m: down_recv.at[m], y)()
    mixed = hidden + (add_slots(down_recv) + vectors[5:6])
    for i in range(2):
        mix_send[i] = mixed[:, LANES * i : LANES * (i + 1)].astype(BF16)
    mix_recv[a] = mix_send[a // 4]
    exchange(21, in_a, lambda p: mix_send.at[p // 4], lambda m: mix_recv.at[m], a)()
    deliver(mix_recv, mixed_out)

    for copy in started:
        copy.wait_send()


STAGES = 22


def local(
    tokens,
    lengths,
    slopes,
    ln1_gain,
    ln1_bias,
    w_qkv,
    b_qkv,
    keys,
    values,
    w_dense,
    b_dense,
    ln2_gain,
    ln2_bias,
    w_up,
    b_up,
    w_down,
    b_down,
):
    count, requests, width = tokens.shape
    features = width * lax.axis_size("seq")
    slot_count = keys.shape[0]
    rows = count * requests

    def as_row(vector):
        return vector.reshape(1, -1)

    bias_blocks = jnp.pad(b_qkv.reshape(6, LANES), ((0, 2), (0, 0)))
    vmem = pl.BlockSpec(memory_space=pltpu.VMEM)
    smem = pl.BlockSpec(memory_space=pltpu.SMEM)
    tile = (GROUP, ROWS, LANES)
    scratch = [
        pltpu.VMEM(tile, BF16),
        pltpu.VMEM(tile, BF16),
        pltpu.VMEM((8, 32), F32),
        pltpu.VMEM((8, LANES), F32),
        pltpu.VMEM((GROUP, 8, LANES), F32),
        pltpu.VMEM((256, 768), BF16),
        pltpu.VMEM((256, 256), BF16),
        pltpu.VMEM((256, 1024), BF16),
        pltpu.VMEM((256, 1024), BF16),
        pltpu.VMEM((1, LANES), F32),
        pltpu.VMEM((GROUP, 1, LANES), F32),
        pltpu.VMEM(tile, F32),
        pltpu.VMEM(tile, F32),
        pltpu.VMEM((ROWS, LANES), BF16),
        pltpu.VMEM(tile, BF16),
        pltpu.VMEM((2, GROUP, ROWS, LANES), BF16),
        pltpu.VMEM((2, rows, slot_count), F32),
        pltpu.VMEM((rows, slot_count), F32),
        pltpu.VMEM((rows, slot_count), BF16),
        pltpu.VMEM((GROUP, ROWS, 256), F32),
        pltpu.VMEM((GROUP, 1, LANES), F32),
        pltpu.VMEM((GROUP, ROWS, 256), F32),
        pltpu.VMEM((GROUP, 1, LANES), F32),
        pltpu.VMEM((GROUP, ROWS, 256), F32),
        pltpu.VMEM((GROUP, 1, LANES), F32),
        pltpu.VMEM((GROUP, ROWS, 256), F32),
        pltpu.VMEM((2, ROWS, LANES), BF16),
        pltpu.VMEM(tile, BF16),
        pltpu.VMEM((1, LANES), F32),
        pltpu.VMEM((GROUP, 1, LANES), F32),
        pltpu.VMEM(tile, F32),
        pltpu.VMEM(tile, F32),
        pltpu.VMEM((ROWS, LANES), BF16),
        pltpu.VMEM(tile, BF16),
        pltpu.VMEM((GROUP, ROWS, 256), F32),
        pltpu.VMEM((2, ROWS, LANES), BF16),
        pltpu.VMEM(tile, BF16),
        pltpu.SemaphoreType.DMA((STAGES, GROUP)),
        pltpu.SemaphoreType.DMA((STAGES, GROUP)),
    ]
    shape = jax.ShapeDtypeStruct((count, width, requests), BF16)

    def body(*refs):
        kernel(features, *refs)

    attended, mixed = pl.pallas_call(
        body,
        out_shape=(shape, shape),
        in_specs=[vmem, vmem, smem] + [vmem] * 14,
        out_specs=(vmem, vmem),
        scratch_shapes=scratch,
        compiler_params=pltpu.CompilerParams(collective_id=0, has_side_effects=True),
        name="layer",
    )(
        tokens.transpose(0, 2, 1),
        as_row(lengths),
        slopes,
        as_row(ln1_gain),
        as_row(ln1_bias),
        w_qkv,
        bias_blocks,
        keys,
        values,
        w_dense.T,
        as_row(b_dense),
        as_row(ln2_gain),
        as_row(ln2_bias),
        w_up,
        b_up.reshape(GROUP, LANES),
        w_down.T,
        as_row(b_down),
    )
    return attended.transpose(0, 2, 1), mixed.transpose(0, 2, 1)


def solution(mesh):
    in_specs = (
        P(None, None, "seq"),
        P(),
        P("mlp"),
        P("seq"),
        P("seq"),
        P("seq", "mlp"),
        P("mlp"),
        P("seq", "mlp"),
        P("seq", "mlp"),
        P("mlp", "seq"),
        P("seq"),
        P("seq"),
        P("seq"),
        P("seq", "mlp"),
        P("mlp"),
        P("mlp", "seq"),
        P("seq"),
    )
    out_specs = (P(None, None, "seq"), P(None, None, "seq"))
    return jax.shard_map(local, mesh=mesh, in_specs=in_specs, out_specs=out_specs, check_vma=False)
```

```python
import math

import jax
import jax.numpy as jnp
from jax import lax
from jax.experimental import pallas as pl
from jax.experimental.pallas import tpu as pltpu
from jax.sharding import PartitionSpec as P

HD = 128
STEPS = 4
GROUP = 8
ROWS = 24
LANES = 128
NEG = -1e30
FLOOR = -1e29
EPS = 1e-05
MESH = pl.DeviceIdType.MESH

F32 = jnp.float32
BF16 = jnp.bfloat16
NT = (((1,), (1,)), ((), ()))


def gelu_tanh(value):
    return (
        0.5
        * value
        * (1.0 + jnp.tanh(0.7978845608028654 * (value + 0.044715 * value * value * value)))
    )


def dot(a, b):
    return jnp.dot(a, b, preferred_element_type=F32)


def dot_nt(a, b):
    return lax.dot_general(a, b, NT, preferred_element_type=F32)


def iota(shape, dim):
    return lax.broadcasted_iota(jnp.int32, shape, dim)


def to_row(columns):
    lane, row = iota((ROWS, LANES), 1), iota((ROWS, LANES), 0)
    packed = jnp.zeros((ROWS, LANES), F32)
    for i, column in enumerate(columns):
        packed = jnp.where(lane == row + 32 * i, column, packed)
    return jnp.sum(packed, axis=0, keepdims=True)


def to_column(row, i):
    lane, place = iota((ROWS, LANES), 1), iota((ROWS, LANES), 0)
    return jnp.sum(jnp.where(lane == place + 32 * i, row, 0.0), axis=1, keepdims=True)


def kernel(
    features,
    tokens,
    lengths,
    slopes,
    ln1_gain,
    ln1_bias,
    w_qkv,
    b_qkv,
    keys_far,
    values_far,
    w_dense,
    b_dense,
    ln2_gain,
    ln2_bias,
    w_up,
    b_up,
    w_down,
    b_down,
    attended_out,
    mixed_out,
    x_send,
    x_recv,
    vec_rows,
    vec_send,
    vec_recv,
    qkv_full,
    dense_full,
    up_full,
    down_full,
    stat_send,
    stat_recv,
    part_qkv,
    sum_qkv,
    own_qkv,
    all_qkv,
    q_all,
    bias,
    score,
    weight,
    o_send,
    ml_send,
    o_recv,
    ml_recv,
    oz_recv,
    mlz_recv,
    dense_recv,
    att_send,
    att_recv,
    part_up,
    sum_up,
    own_act,
    all_act,
    down_recv,
    mix_send,
    mix_recv,
    keys,
    values,
    send_sem,
    recv_sem,
    load_sem,
):
    rows = ROWS * GROUP
    requests = lengths.shape[1]
    slot_count = keys.shape[0]
    s = lax.axis_index("seq")
    y = lax.axis_index("mlp")
    z, a = s // GROUP, lax.rem(s, GROUP)

    def in_a(k):
        peer = lax.rem(a + k, GROUP)
        return peer, (z * GROUP + peer, y)

    def in_z(k):
        peer = lax.rem(z + k, GROUP)
        return peer, (peer * GROUP + a, y)

    def in_y(k):
        peer = lax.rem(y + k, GROUP)
        return peer, (s, peer)

    barrier = pltpu.get_barrier_semaphore()
    for ring in (in_a, in_z, in_y):
        for k in range(1, GROUP):
            pl.semaphore_signal(barrier, inc=1, device_id=ring(k)[1], device_id_type=MESH)

    started = []

    def exchange(stage, ring, source, target, me):
        copies = []
        for k in range(1, GROUP):
            peer, device = ring(k)
            copy = pltpu.make_async_remote_copy(
                src_ref=source(peer),
                dst_ref=target(me),
                send_sem=send_sem.at[stage, k],
                recv_sem=recv_sem.at[stage, k],
                device_id=device,
                device_id_type=MESH,
            )
            copy.start()
            copies.append(copy)
        started.extend(copies)

        def arrived():
            for copy in copies:
                copy.wait_recv()

        return arrived

    own = pl.ds(pl.multiple_of(a * 32, 32), 32)
    loads = []
    for i, (source, target) in enumerate(
        (
            (w_dense, dense_full.at[own, :]),
            (w_up, up_full.at[own, :]),
            (w_down, down_full.at[own, :]),
            (keys_far, keys),
            (values_far, values),
        )
    ):
        load = pltpu.make_async_copy(source, target, load_sem.at[i])
        load.start()
        loads.append(load)

    quarter = lax.rem(a, 4)
    spread = (iota((32, LANES), 1) == iota((32, LANES), 0) + 32 * quarter).astype(BF16)
    mine = jnp.zeros((rows, 32), F32)
    for t in range(STEPS):
        pick = (iota((rows, requests), 0) == STEPS * iota((rows, requests), 1) + t).astype(BF16)
        mine += dot_nt(pick, tokens[t])
    placed = dot(mine.astype(BF16), spread).astype(BF16).astype(F32)
    for b in range(GROUP):
        x_send[b] = placed[ROWS * b : ROWS * (b + 1)].astype(BF16)
    x_recv[a] = x_send[a]

    vec_rows[...] = jnp.zeros_like(vec_rows)
    for i, ref in enumerate((ln1_gain, ln1_bias, ln2_gain, ln2_bias, b_dense, b_down)):
        vec_rows[i : i + 1, :] = ref[...]
    vec_send[...] = jnp.dot(
        vec_rows[...],
        (iota((32, LANES), 1) == iota((32, LANES), 0) + 32 * quarter).astype(F32),
        preferred_element_type=F32,
        precision=lax.Precision.HIGHEST,
    )
    vec_recv[a] = vec_send[...]

    def block_of(ref):
        def at(i):
            return ref.at[pl.ds(pl.multiple_of(i * 32, 32), 32), :]

        return at

    qkv_full[own, :] = w_qkv[...]

    pl.semaphore_wait(barrier, 3 * (GROUP - 1))

    x_here = exchange(0, in_a, lambda p: x_send.at[p], lambda m: x_recv.at[m], a)
    vec_here = exchange(1, in_a, lambda p: vec_send, lambda m: vec_recv.at[m], a)
    qkv_here = exchange(2, in_a, lambda p: w_qkv, block_of(qkv_full), a)
    loads[0].wait()
    dense_here = exchange(3, in_a, lambda p: dense_full.at[own, :], block_of(dense_full), a)
    loads[1].wait()
    up_here = exchange(4, in_a, lambda p: up_full.at[own, :], block_of(up_full), a)
    loads[2].wait()
    down_here = exchange(5, in_a, lambda p: down_full.at[own, :], block_of(down_full), a)

    def halves(slots):
        low = slots[0].astype(F32)
        high = slots[4].astype(F32)
        for i in range(1, 4):
            low = low + slots[i].astype(F32)
            high = high + slots[4 + i].astype(F32)
        return jnp.concatenate([low, high], axis=1)

    def statistics(tile):
        return to_row(
            [jnp.sum(tile, axis=1, keepdims=True), jnp.sum(tile * tile, axis=1, keepdims=True)]
        )

    def add_slots(slots):
        total = slots[0].astype(F32)
        for i in range(1, GROUP):
            total = total + slots[i].astype(F32)
        return total

    def normalize(tile, stats, gain, shift):
        mean = to_column(stats, 0) / features
        spread = to_column(stats, 1) / features - mean * mean
        return ((tile - mean) * lax.rsqrt(spread + EPS) * gain + shift).astype(BF16)

    half = 32
    position = (s * slot_count + iota((1, slot_count), 1)).astype(F32)
    for c in range(rows // half):
        row = iota((half, 1), 0) + half * c
        request, step = row >> 2, (row & 3).astype(F32)
        lane = iota((half, requests), 1)
        cached = jnp.broadcast_to(lengths[...], (half, requests)).astype(F32)
        start = jnp.sum(jnp.where(lane < request, cached + STEPS, 0.0), axis=1, keepdims=True)
        length = jnp.sum(jnp.where(lane == request, cached, 0.0), axis=1, keepdims=True)
        offset = position - start
        valid = (offset >= 0.0) & (offset < length)
        distance = (length + step) - offset
        for h in range(2):
            bias[h, half * c : half * (c + 1), :] = jnp.where(valid, -slopes[h] * distance, NEG)

    x_here()
    x = halves(x_recv)
    stat_send[...] = statistics(x)
    stat_recv[z] = stat_send[...]
    stat_here = exchange(6, in_z, lambda p: stat_send, lambda m: stat_recv.at[m], z)

    vec_here()
    vectors = halves(vec_recv)
    stat_here()
    normed = normalize(x, add_slots(stat_recv), vectors[0:1], vectors[1:2])

    qkv_here()
    partial = dot(normed, qkv_full[...])
    for j in range(6):
        part_qkv[j] = partial[:, LANES * j : LANES * (j + 1)]
    for j in range(6, GROUP):
        part_qkv[j] = jnp.zeros((ROWS, LANES), F32)
    sum_qkv[z] = part_qkv[z]
    exchange(7, in_z, lambda p: part_qkv.at[p], lambda m: sum_qkv.at[m], z)()
    own_qkv[...] = (add_slots(sum_qkv) + b_qkv[pl.ds(jnp.minimum(z, 5), 1), :]).astype(BF16)
    all_qkv[z] = own_qkv[...]
    exchange(8, in_z, lambda p: own_qkv, lambda m: all_qkv.at[m], z)()
    for h in range(2):
        q_all[h, a] = all_qkv[3 * h]
    q0_here = exchange(9, in_a, lambda p: all_qkv.at[0], lambda m: q_all.at[0, m], a)
    q1_here = exchange(10, in_a, lambda p: all_qkv.at[3], lambda m: q_all.at[1, m], a)

    scale = 1.0 / math.sqrt(HD)
    fresh = []
    one, other = iota((ROWS, ROWS), 0), iota((ROWS, ROWS), 1)
    seen = ((one >> 2) == (other >> 2)) & ((other & 3) <= (one & 3))
    gap = ((one & 3) - (other & 3)).astype(F32)
    for h in range(2):
        near = dot_nt(all_qkv[3 * h], all_qkv[3 * h + 1]) * scale - slopes[h] * gap
        near = jnp.where(seen, near, NEG)
        top = jnp.max(near, axis=1, keepdims=True)
        share = jnp.exp(near - top)
        fresh.append(
            (dot(share.astype(BF16), all_qkv[3 * h + 2]), top, jnp.sum(share, axis=1, keepdims=True))
        )

    loads[3].wait()
    loads[4].wait()
    maxima, totals = [], []
    for h in range(2):
        (q0_here, q1_here)[h]()
        query = q_all[h].astype(F32).reshape(rows, HD).astype(BF16)
        score[...] = dot_nt(query, keys[:, HD * h : HD * (h + 1)])
        tops, sums = [], []
        for c in range(rows // half):
            span = slice(half * c, half * (c + 1))
            value = score[span, :] * scale + bias[h, span, :]
            top = jnp.maximum(jnp.max(value, axis=1, keepdims=True), FLOOR)
            share = jnp.exp(value - top)
            weight[span, :] = share.astype(BF16)
            tops.append(top)
            sums.append(jnp.sum(share, axis=1, keepdims=True))
        maxima.append(jnp.concatenate(tops, axis=0))
        totals.append(jnp.concatenate(sums, axis=0))
        out = dot(weight[...], values[:, HD * h : HD * (h + 1)])
        for b in range(GROUP):
            o_send[b, :, HD * h : HD * (h + 1)] = out[ROWS * b : ROWS * (b + 1)].astype(BF16)
    for b in range(GROUP):
        span = slice(ROWS * b, ROWS * (b + 1))
        ml_send[b] = to_row([maxima[0][span], maxima[1][span], totals[0][span], totals[1][span]])
    o_recv[a] = o_send[a]
    ml_recv[a] = ml_send[a]
    ml_here = exchange(11, in_a, lambda p: ml_send.at[p], lambda m: ml_recv.at[m], a)
    o_here = exchange(12, in_a, lambda p: o_send.at[p], lambda m: o_recv.at[m], a)

    def combine(parts):
        top = parts[0][1]
        for part in parts[1:]:
            top = jnp.maximum(top, part[1])
        weighted, total = 0.0, 0.0
        for value, largest, amount in parts:
            factor = jnp.exp(largest - top)
            weighted = weighted + value * factor
            total = total + amount * factor
        return weighted, top, total

    def slots_of(o_ref, ml_ref, h):
        return [
            (
                o_ref[i, :, HD * h : HD * (h + 1)].astype(F32),
                to_column(ml_ref[i], h),
                to_column(ml_ref[i], 2 + h),
            )
            for i in range(GROUP)
        ]

    ml_here()
    o_here()
    merged = [combine(slots_of(o_recv, ml_recv, h)) for h in range(2)]
    for h in range(2):
        oz_recv[z, :, HD * h : HD * (h + 1)] = merged[h][0].astype(BF16)
    mlz_recv[z] = to_row([merged[0][1], merged[1][1], merged[0][2], merged[1][2]])
    ml_here = exchange(13, in_z, lambda p: mlz_recv.at[z], lambda m: mlz_recv.at[m], z)
    o_here = exchange(14, in_z, lambda p: oz_recv.at[z], lambda m: oz_recv.at[m], z)
    ml_here()
    o_here()
    attention = []
    for h in range(2):
        weighted, _, total = combine(slots_of(oz_recv, mlz_recv, h) + [fresh[h]])
        attention.append((weighted / total).astype(BF16))
    attention = jnp.concatenate(attention, axis=1)

    dense_here()
    dense_recv[y] = dot_nt(attention, dense_full[...]).astype(BF16)
    exchange(15, in_y, lambda p: dense_recv.at[y], lambda m: dense_recv.at[m], y)()
    dense = add_slots(dense_recv) + vectors[4:5]
    hidden = (x + dense).astype(BF16).astype(F32)

    up_here()
    gain, shift = vectors[2:3], vectors[3:4]
    left = jnp.concatenate([hidden * gain, gain, shift, jnp.zeros((6, gain.shape[1]), F32)], axis=0)
    coarse = left.astype(BF16)
    fine = (left - coarse.astype(F32)).astype(BF16)
    partial = dot(coarse, up_full[...]) + dot(fine, up_full[...])
    last = iota((8, LANES), 0)
    sums = statistics(hidden)
    for j in range(GROUP):
        block = partial[:, LANES * j : LANES * (j + 1)]
        part_up[j, 0:ROWS] = block[:ROWS]
        part_up[j, ROWS : ROWS + 8] = jnp.where(last == 2, sums, block[ROWS:])
    sum_up[z] = part_up[z]
    sum_here = exchange(18, in_z, lambda p: part_up.at[p], lambda m: sum_up.at[m], z)
    for i in range(2):
        att_send[i] = dense[:, LANES * i : LANES * (i + 1)].astype(BF16)
    att_recv[a] = att_send[a // 4]
    att_here = exchange(17, in_a, lambda p: att_send.at[p // 4], lambda m: att_recv.at[m], a)
    sum_here()
    total = add_slots(sum_up)
    gained, shifted, stats = (total[ROWS + i : ROWS + i + 1] for i in range(3))
    mean = to_column(stats, 0) / features
    variance = to_column(stats, 1) / features - mean * mean
    upward = lax.rsqrt(variance + EPS) * (total[:ROWS] - mean * gained) + shifted
    own_act[...] = gelu_tanh(upward + b_up[pl.ds(z, 1), :]).astype(BF16)
    all_act[z] = own_act[...]
    act_here = exchange(19, in_z, lambda p: own_act, lambda m: all_act.at[m], z)

    def deliver(slots, out_ref):
        held = jnp.concatenate([slots[i].astype(F32) for i in range(GROUP)], axis=0)
        own = dot_nt(spread, held.astype(BF16)).astype(BF16)
        for t in range(STEPS):
            put = iota((rows, requests), 0) == STEPS * iota((rows, requests), 1) + t
            out_ref[t] = dot(own, put.astype(BF16)).astype(BF16)

    att_here()
    deliver(att_recv, attended_out)

    down_here()
    act_here()
    act = jnp.concatenate([all_act[i] for i in range(GROUP)], axis=1)
    down_recv[y] = dot_nt(act, down_full[...]).astype(BF16)
    exchange(20, in_y, lambda p: down_recv.at[y], lambda m: down_recv.at[m], y)()
    mixed = hidden + (add_slots(down_recv) + vectors[5:6])
    for i in range(2):
        mix_send[i] = mixed[:, LANES * i : LANES * (i + 1)].astype(BF16)
    mix_recv[a] = mix_send[a // 4]
    exchange(21, in_a, lambda p: mix_send.at[p // 4], lambda m: mix_recv.at[m], a)()
    deliver(mix_recv, mixed_out)

    for copy in started:
        copy.wait_send()


STAGES = 22


def local(
    tokens,
    lengths,
    slopes,
    ln1_gain,
    ln1_bias,
    w_qkv,
    b_qkv,
    keys,
    values,
    w_dense,
    b_dense,
    ln2_gain,
    ln2_bias,
    w_up,
    b_up,
    w_down,
    b_down,
):
    count, requests, width = tokens.shape
    features = width * lax.axis_size("seq")
    slot_count = keys.shape[0]
    rows = count * requests

    def as_row(vector):
        return vector.reshape(1, -1)

    vmem = pl.BlockSpec(memory_space=pltpu.VMEM)
    smem = pl.BlockSpec(memory_space=pltpu.SMEM)
    far = pl.BlockSpec(memory_space=pl.ANY)
    tile = (GROUP, ROWS, LANES)
    scratch = [
        pltpu.VMEM(tile, BF16),
        pltpu.VMEM(tile, BF16),
        pltpu.VMEM((8, 32), F32),
        pltpu.VMEM((8, LANES), F32),
        pltpu.VMEM((GROUP, 8, LANES), F32),
        pltpu.VMEM((256, 768), BF16),
        pltpu.VMEM((256, 256), BF16),
        pltpu.VMEM((256, 1024), BF16),
        pltpu.VMEM((256, 1024), BF16),
        pltpu.VMEM((1, LANES), F32),
        pltpu.VMEM((GROUP, 1, LANES), F32),
        pltpu.VMEM(tile, F32),
        pltpu.VMEM(tile, F32),
        pltpu.VMEM((ROWS, LANES), BF16),
        pltpu.VMEM(tile, BF16),
        pltpu.VMEM((2, GROUP, ROWS, LANES), BF16),
        pltpu.VMEM((2, rows, slot_count), F32),
        pltpu.VMEM((rows, slot_count), F32),
        pltpu.VMEM((rows, slot_count), BF16),
        pltpu.VMEM((GROUP, ROWS, 256), BF16),
        pltpu.VMEM((GROUP, 1, LANES), F32),
        pltpu.VMEM((GROUP, ROWS, 256), BF16),
        pltpu.VMEM((GROUP, 1, LANES), F32),
        pltpu.VMEM((GROUP, ROWS, 256), BF16),
        pltpu.VMEM((GROUP, 1, LANES), F32),
        pltpu.VMEM((GROUP, ROWS, 256), BF16),
        pltpu.VMEM((2, ROWS, LANES), BF16),
        pltpu.VMEM(tile, BF16),
        pltpu.VMEM((GROUP, ROWS + 8, LANES), F32),
        pltpu.VMEM((GROUP, ROWS + 8, LANES), F32),
        pltpu.VMEM((ROWS, LANES), BF16),
        pltpu.VMEM(tile, BF16),
        pltpu.VMEM((GROUP, ROWS, 256), BF16),
        pltpu.VMEM((2, ROWS, LANES), BF16),
        pltpu.VMEM(tile, BF16),
        pltpu.VMEM((slot_count, 256), BF16),
        pltpu.VMEM((slot_count, 256), BF16),
        pltpu.SemaphoreType.DMA((STAGES, GROUP)),
        pltpu.SemaphoreType.DMA((STAGES, GROUP)),
        pltpu.SemaphoreType.DMA((5,)),
    ]
    shape = jax.ShapeDtypeStruct((count, width, requests), BF16)

    def body(*refs):
        kernel(features, *refs)

    attended, mixed = pl.pallas_call(
        body,
        out_shape=(shape, shape),
        in_specs=[vmem, vmem, smem] + [vmem] * 4 + [far] * 3 + [vmem] * 3 + [far] + [vmem] + [far] + [vmem],
        out_specs=(vmem, vmem),
        scratch_shapes=scratch,
        compiler_params=pltpu.CompilerParams(collective_id=0, has_side_effects=True),
        name="layer",
    )(
        tokens.transpose(0, 2, 1),
        as_row(lengths),
        slopes,
        as_row(ln1_gain),
        as_row(ln1_bias),
        w_qkv,
        b_qkv.reshape(6, LANES),
        keys,
        values,
        w_dense.T,
        as_row(b_dense),
        as_row(ln2_gain),
        as_row(ln2_bias),
        w_up,
        b_up.reshape(GROUP, LANES),
        w_down.T,
        as_row(b_down),
    )
    return attended.transpose(0, 2, 1), mixed.transpose(0, 2, 1)


def solution(mesh):
    in_specs = (
        P(None, None, "seq"),
        P(),
        P("mlp"),
        P("seq"),
        P("seq"),
        P("seq", "mlp"),
        P("mlp"),
        P("seq", "mlp"),
        P("seq", "mlp"),
        P("mlp", "seq"),
        P("seq"),
        P("seq"),
        P("seq"),
        P("seq", "mlp"),
        P("mlp"),
        P("mlp", "seq"),
        P("seq"),
    )
    out_specs = (P(None, None, "seq"), P(None, None, "seq"))
    return jax.shard_map(local, mesh=mesh, in_specs=in_specs, out_specs=out_specs, check_vma=False)
```
